256 devices in a mesh: pipe: 4 (over x), dom: 64 (over y, z, core).
Axes of the slice: x: 4, y: 4, z: 8, core: 2. Of those that a mesh axis runs over, the one named last changes fastest.
Arguments:
- node_states: bfloat16 [4, 1, 4096, 512], P('pipe', None, 'dom'), may hold values from -6 to 6
- edge_states: bfloat16 [4, 1, 16384, 512], P('pipe', None, 'dom'), may hold values from -6 to 6
- node_cot: bfloat16 [1, 4096, 512], P(None, 'dom'), may hold values from -6 to 6
- edge_cot: bfloat16 [1, 16384, 512], P(None, 'dom'), may hold values from -6 to 6
- edge_w1: bfloat16 [4, 1536, 512], P('pipe'), may hold values from -0.15625 to 0.15625
- edge_w2: bfloat16 [4, 512, 512], P('pipe'), may hold values from -0.25 to 0.25
- edge_gain: bfloat16 [4, 512], P('pipe'), may hold values from 0.5 to 1.5
- node_w1: bfloat16 [4, 1024, 512], P('pipe'), may hold values from -0.1875 to 0.1875
- node_w2: bfloat16 [4, 512, 512], P('pipe'), may hold values from -0.25 to 0.25
- node_gain: bfloat16 [4, 512], P('pipe'), may hold values from 0.5 to 1.5
- edge_src: int32 [16384], P('dom'), may hold values from 0 to 191, as said below
- edge_dst: int32 [16384], P('dom'), may hold values from 0 to 63
- edge_count: int32 [64], P('dom'), may hold values from 128 to 256, as said below
- send_rows: int32 [64, 64, 2], P('dom'), may hold values from 0 to 63
Outputs:
- node_grads: bfloat16 [4, 1, 4096, 512], P('pipe', None, 'dom')
- edge_grads: bfloat16 [4, 1, 16384, 512], P('pipe', None, 'dom')
- edge_w1_grad: float32 [4, 1536, 512], P('pipe', 'dom')
- edge_w2_grad: float32 [4, 512, 512], P('pipe', 'dom')
- edge_gain_grad: float32 [4, 512], P('pipe', 'dom')
- node_w1_grad: float32 [4, 1024, 512], P('pipe', 'dom')
- node_w2_grad: float32 [4, 512, 512], P('pipe', 'dom')
- node_gain_grad: float32 [4, 512], P('pipe', 'dom')
The draws below stay inside these ranges and needn't reach their ends.
Inputs may be any that keep to these rules, and one draw needn't show every extreme that they name: `edge_src`: each partition's edges name its own nodes below 64 and its received rows from 64 on; every received row is the sender of some live edge of its partition. `edge_count`: some partition has all 256 edges live in every draw.
All inputs are finite; a program needn't handle non-finite values.
Results may differ from the reference program's by a relative error of at most 0.04.
Values may be sent and summed in bfloat16 or wider, within the bound.
A program may use at most 64 MiB of HBM per device.

```python
import jax
import jax.numpy as jnp
from jax import lax

D = 512
HID = 512
N_DEV = 64
E_CAP = 256
MICRO = 1
SLOT = 2
PARTITIONS = 64
SECTIONS = 4
GHOSTS = 128
NODES = 4096
EDGES = 16384


def draw_edge_src(key, part):

    def one_partition(sub_key):
        base = jax.random.randint(jax.random.fold_in(sub_key, 1), (E_CAP,), 0, N_DEV + GHOSTS)
        places = jax.random.permutation(jax.random.fold_in(sub_key, 2), E_CAP // 2)[:GHOSTS]
        return base.at[places].set(N_DEV + jnp.arange(GHOSTS, dtype=jnp.int32))
    keys = jax.vmap(lambda index: jax.random.fold_in(key, index))(jnp.arange(PARTITIONS))
    return jax.vmap(one_partition)(keys).reshape(-1).astype(jnp.int32)


def draw_edge_count(key, part):
    counts = E_CAP // 2 + jax.random.randint(jax.random.fold_in(key, 11), (PARTITIONS,), 0, E_CAP // 2 + 1)
    busiest = jax.random.randint(jax.random.fold_in(key, 12), (), 0, PARTITIONS)
    return counts.at[busiest].set(E_CAP).astype(jnp.int32)


def plant(values, stream_key, least, largest):
    place = [jax.random.randint(jax.random.fold_in(stream_key, axis), (), 0, length) for axis, length in enumerate(values.shape)]
    widest = values.shape.index(max(values.shape))
    beside = place[:widest] + [(place[widest] + 1) % values.shape[widest]] + place[widest + 1:]
    return values.at[tuple(place)].set(least).at[tuple(beside)].set(largest)


def level_of(key, extent, pieces, low, high):
    factor_of, own = 1.0, jax.random.fold_in(key, 6)
    for dim, blocks in pieces:
        steps = jnp.exp(jax.random.uniform(jax.random.fold_in(own, dim), (blocks,), jnp.float32, low / len(pieces), high / len(pieces)))
        factor_of = factor_of * jnp.repeat(steps, extent[dim] // blocks).reshape([-1 if axis == dim else 1 for axis in range(len(extent))])
    return factor_of


def gaussian(own_key, extent, scale, bound, split=(), kind=jnp.bfloat16):
    drawn = jax.random.normal(own_key, extent, jnp.float32) * scale
    if len(split) > 0:
        drawn = level_of(own_key, extent, split, -0.22, 0.18) * drawn
    return jnp.clip(drawn, min=-bound, max=bound).astype(kind)


def setup_inputs(seed: int = 0) -> dict:
    key_list = jax.random.split(jax.random.key(seed), 15)
    node_states = gaussian(key_list[0], (SECTIONS, MICRO, NODES, D), 1.0, 6.0, ((0, 4), (2, 64)))
    edge_states = gaussian(key_list[1], (SECTIONS, MICRO, EDGES, D), 1.0, 6.0, ((0, 4), (2, 64)))
    node_cot = gaussian(key_list[2], (MICRO, NODES, D), 1.0, 6.0, ((1, 64),))
    edge_cot = gaussian(key_list[3], (MICRO, EDGES, D), 1.0, 6.0, ((1, 64),))
    edge_w1 = gaussian(key_list[4], (SECTIONS, 3 * D, HID), (3 * D) ** -0.5, 0.15625, ((0, 4),))
    edge_w2 = gaussian(key_list[5], (SECTIONS, HID, D), HID ** -0.5, 0.25, ((0, 4),))
    edge_gain = jnp.clip(1.0 + 0.1 * jax.random.normal(key_list[6], (SECTIONS, D), jnp.float32), 0.5, 1.5).astype(jnp.bfloat16)
    node_w1 = gaussian(key_list[7], (SECTIONS, 2 * D, HID), (2 * D) ** -0.5, 0.1875, ((0, 4),))
    node_w2 = gaussian(key_list[8], (SECTIONS, HID, D), HID ** -0.5, 0.25, ((0, 4),))
    node_gain = jnp.clip(1.0 + 0.1 * jax.random.normal(key_list[9], (SECTIONS, D), jnp.float32), 0.5, 1.5).astype(jnp.bfloat16)
    edge_src = draw_edge_src(jax.random.fold_in(key_list[14], 71), 0)
    edge_dst = plant(jax.random.randint(key_list[11], (EDGES,), 0, N_DEV), jax.random.fold_in(key_list[11], 1), 0, N_DEV - 1).astype(jnp.int32)
    edge_count = draw_edge_count(jax.random.fold_in(key_list[14], 71), 0)
    send_rows = plant(jax.random.randint(key_list[13], (PARTITIONS, PARTITIONS, SLOT), 0, N_DEV), jax.random.fold_in(key_list[13], 1), 0, N_DEV - 1).astype(jnp.int32)
    return dict(node_states=node_states, edge_states=edge_states, node_cot=node_cot, edge_cot=edge_cot, edge_w1=edge_w1, edge_w2=edge_w2, edge_gain=edge_gain, node_w1=node_w1, node_w2=node_w2, node_gain=node_gain, edge_src=edge_src, edge_dst=edge_dst, edge_count=edge_count, send_rows=send_rows)


EPS = 1e-05

def contract(former, latter):
    return lax.dot_general(former, latter, (((0,), (0,)), ((), ())), preferred_element_type=jnp.float32)

def mlp_forward(inputs, inner_weight, outer_weight):
    hidden_pre = jnp.dot(inputs, inner_weight, preferred_element_type=jnp.float32)
    hidden_act = jax.nn.silu(hidden_pre).astype(jnp.bfloat16)
    output = jnp.dot(hidden_act, outer_weight, preferred_element_type=jnp.float32)
    centred = output - lax.optimization_barrier(jnp.mean(output, axis=-1, keepdims=True))
    rescale = lax.rsqrt(lax.optimization_barrier(jnp.mean(centred * centred, axis=-1, keepdims=True)) + EPS)
    return (hidden_pre, hidden_act, centred * rescale, rescale)

def mlp_backward(inner_weight, outer_weight, gain_vector, stored, cotangent):
    hidden_pre, hidden_act, normed, rescale = stored
    grad_norm = cotangent * gain_vector.astype(jnp.float32)
    grad_out = rescale * (grad_norm - lax.optimization_barrier(jnp.mean(grad_norm, axis=-1, keepdims=True)) - normed * lax.optimization_barrier(jnp.mean(grad_norm * normed, axis=-1, keepdims=True)))
    grad_out = grad_out.astype(jnp.bfloat16)
    grad_act = jnp.dot(grad_out, outer_weight.T, preferred_element_type=jnp.float32)
    logistic = jax.nn.sigmoid(hidden_pre)
    grad_pre = (grad_act * logistic * (1.0 + hidden_pre * (1.0 - logistic))).astype(jnp.bfloat16)
    grad_in = jnp.dot(grad_pre, inner_weight.T, preferred_element_type=jnp.float32)
    return (grad_in, hidden_act, grad_out, grad_pre, lax.optimization_barrier(jnp.sum(cotangent * normed, axis=0)))

def layer_backward(node_rows, source_rows, edge_rows, receiver, live_mask, node_cotan, edge_cotan, params):
    edge_inner, edge_outer, edge_scale, node_inner, node_outer, node_scale = params
    count_nodes = node_rows.shape[0]
    width = node_rows.shape[1]
    edge_input = jnp.concatenate([edge_rows, source_rows, node_rows[receiver]], axis=1)
    edge_stored = mlp_forward(edge_input, edge_inner, edge_outer)
    new_edges = edge_rows.astype(jnp.float32) + edge_stored[2] * edge_scale.astype(jnp.float32)
    aggregate = jax.ops.segment_sum(new_edges * live_mask[:, None], receiver, num_segments=count_nodes)
    node_input = jnp.concatenate([node_rows, aggregate.astype(jnp.bfloat16)], axis=1)
    node_stored = mlp_forward(node_input, node_inner, node_outer)
    node_back = mlp_backward(node_inner, node_outer, node_scale, node_stored, node_cotan.astype(jnp.float32))
    node_grad_in = node_back[0]
    grad_edges = (edge_cotan.astype(jnp.float32) + node_grad_in[:, width:][receiver]) * live_mask[:, None]
    edge_back = mlp_backward(edge_inner, edge_outer, edge_scale, edge_stored, grad_edges)
    edge_grad_in = edge_back[0]
    edge_result = (grad_edges + edge_grad_in[:, :width]).astype(jnp.bfloat16)
    node_partial = node_cotan.astype(jnp.float32) + node_grad_in[:, :width] + jax.ops.segment_sum(edge_grad_in[:, 2 * width:], receiver, num_segments=count_nodes)
    return (node_partial, edge_grad_in[:, width:2 * width], edge_result, (edge_input,) + tuple(edge_back[1:]), (node_input,) + tuple(node_back[1:]))

def weight_terms(edge_terms, node_terms):
    result = ()
    for terms in (edge_terms, node_terms):
        inputs, hidden_act, grad_out, grad_pre, gain_sum = terms
        result = result + (contract(inputs, grad_pre), contract(hidden_act, grad_out), gain_sum)
    return result

def reference(node_states, edge_states, node_cot, edge_cot, edge_w1, edge_w2, edge_gain, node_w1, node_w2, node_gain, edge_src, edge_dst, edge_count, send_rows):
    position = jnp.arange(EDGES, dtype=jnp.int32)
    owner = position // E_CAP
    local_position = position % E_CAP
    ghost = jnp.maximum(edge_src - N_DEV, 0)
    peer = ghost // SLOT
    column = ghost % SLOT
    remote = peer * N_DEV + send_rows[peer, owner, column]
    source = jnp.where(edge_src < N_DEV, owner * N_DEV + edge_src, remote).astype(jnp.int32)
    receiver = (owner * N_DEV + edge_dst).astype(jnp.int32)
    live_mask = (local_position < edge_count[owner]).astype(jnp.float32)
    node_lists = [[None] * MICRO for section in range(SECTIONS)]
    edge_lists = [[None] * MICRO for section in range(SECTIONS)]
    totals = []
    for section in range(SECTIONS):
        params = (edge_w1[section], edge_w2[section], edge_gain[section], node_w1[section], node_w2[section], node_gain[section])
        totals.append(tuple((jnp.zeros(weight.shape, jnp.float32) for weight in params)))
    for batch_index in range(MICRO):
        node_cotan = node_cot[batch_index]
        edge_cotan = edge_cot[batch_index]
        for section in range(SECTIONS - 1, -1, -1):
            params = (edge_w1[section], edge_w2[section], edge_gain[section], node_w1[section], node_w2[section], node_gain[section])
            node_rows = node_states[section, batch_index]
            node_partial, source_grads, edge_result, edge_terms, node_terms = layer_backward(node_rows, node_rows[source], edge_states[section, batch_index], receiver, live_mask, node_cotan, edge_cotan, params)
            node_result = (node_partial + jax.ops.segment_sum(source_grads, source, num_segments=NODES)).astype(jnp.bfloat16)
            terms = weight_terms(edge_terms, node_terms)
            totals[section] = tuple((total + term for total, term in zip(totals[section], terms)))
            node_lists[section][batch_index] = node_result
            edge_lists[section][batch_index] = edge_result
            node_cotan = node_result
            edge_cotan = edge_result
    node_grads = jnp.stack([jnp.stack(row) for row in node_lists])
    edge_grads = jnp.stack([jnp.stack(row) for row in edge_lists])
    stacked = [jnp.stack([totals[section][which] for section in range(SECTIONS)]) for which in range(6)]
    return (node_grads, edge_grads, stacked[0], stacked[1], stacked[2], stacked[3], stacked[4], stacked[5])
```

```python
import functools

import jax
import jax.numpy as jnp
from jax import lax
from jax.experimental import pallas as pl
from jax.experimental.pallas import tpu as pltpu
from jax.sharding import PartitionSpec as P

EPS = 1e-05
MESH = pl.DeviceIdType.MESH
F32 = jnp.float32
BF16 = jnp.bfloat16
DOM_Z = 8
DOM_CORE = 2


def passed_along(value, axis, steps):
    count = lax.axis_size(axis)
    first, last = (max(0, -steps), min(count, count - steps))
    return lax.ppermute(value, axis, [(source, source + steps) for source in range(first, last)])


def dot(a, b):
    return jnp.dot(a, b, preferred_element_type=F32)


def dot_t(a, b):
    return lax.dot_general(a, b, (((1,), (1,)), ((), ())), preferred_element_type=F32)


def contract(a, b):
    return lax.dot_general(a, b, (((0,), (0,)), ((), ())), preferred_element_type=F32)


def mean(x):
    return jnp.mean(x, axis=-1, keepdims=True)


def mlp_forward(pre, outer):
    sig = jax.nn.sigmoid(pre)
    act = (pre * sig).astype(BF16)
    out = dot(act, outer)
    centred = out - mean(out)
    rescale = lax.rsqrt(mean(centred * centred) + EPS)
    slope = sig * (1.0 + pre * (1.0 - sig))
    return act, slope, centred * rescale, rescale


def mlp_backward(outer, gain, slope, normed, rescale, cotangent):
    grad_norm = cotangent * gain
    grad_out = rescale * (grad_norm - mean(grad_norm) - normed * mean(grad_norm * normed))
    grad_out = grad_out.astype(BF16)
    grad_pre = (dot_t(grad_out, outer) * slope).astype(BF16)
    return grad_out, grad_pre, jnp.sum(cotangent * normed, axis=0, keepdims=True)


def reduce_kernel(
    dims,
    x_e, pre_e, act_e, out_e, x_n, pre_n, act_n, out_n, gains,
    w1e, w2e, ge, w1n, w2n, gn,
    terms, from_core, chip_sum, from_y, y_sum, from_z,
    sem_core_s, sem_core_r, sem_y_s, sem_y_r, sem_z_s, sem_z_r,
):
    ny, nz = dims
    dom = lax.axis_index("dom")
    core = lax.rem(dom, 2)
    z = lax.rem(lax.div(dom, 2), nz)
    y = lax.div(dom, 2 * nz)

    def at(yy, zz, cc):
        return {"dom": (yy * nz + zz) * 2 + cc}

    barrier = pltpu.get_barrier_semaphore()
    pl.semaphore_signal(barrier, inc=1, device_id=at(y, z, 1 - core), device_id_type=MESH)
    for k in range(1, ny):
        pl.semaphore_signal(
            barrier, inc=1, device_id=at(lax.rem(y + k, ny), z, core), device_id_type=MESH
        )
    for k in range(1, nz):
        pl.semaphore_signal(
            barrier, inc=1, device_id=at(y, lax.rem(z + k, nz), core), device_id_type=MESH
        )

    count = ny * nz * 2
    a1 = w1e.shape[0]
    b1 = w1n.shape[0]
    e1 = contract(x_e[...], pre_e[...])
    e2 = contract(act_e[...], out_e[...])
    n1 = contract(x_n[...], pre_n[...])
    n2 = contract(act_n[...], out_n[...])
    a2 = e2.shape[0] // count
    b2 = n2.shape[0] // count
    gain_rows = gains[...]
    ra = a1 + a2
    rb = ra + b1
    for d in range(count):
        c, yz = d % 2, d // 2
        yy, zz = yz // nz, yz % nz
        terms[c, zz, yy, 0:ra] = jnp.concatenate(
            [e1[a1 * d : a1 * d + a1], e2[a2 * d : a2 * d + a2]], axis=0
        ).astype(BF16)
        terms[c, zz, yy, ra:rb] = n1[b1 * d : b1 * d + b1].astype(BF16)
        terms[c, zz, yy, rb : rb + b2 + 8] = jnp.concatenate(
            [n2[b2 * d : b2 * d + b2], gain_rows], axis=0
        ).astype(BF16)

    pl.semaphore_wait(barrier, ny + nz - 1)

    order = sorted(range(nz), key=lambda k: -min(k, nz - k))
    places = [lax.rem(z + k, nz) for k in order]
    core_copies, y_copies, z_copies = [], [], []
    for i, place in enumerate(places):
        copy = pltpu.make_async_remote_copy(
            src_ref=terms.at[1 - core, place],
            dst_ref=from_core.at[place],
            send_sem=sem_core_s.at[i],
            recv_sem=sem_core_r.at[place],
            device_id=at(y, z, 1 - core),
            device_id_type=MESH,
        )
        copy.start()
    for i, place in enumerate(places):
        pltpu.make_async_remote_copy(
            src_ref=terms.at[1 - core, place],
            dst_ref=from_core.at[place],
            send_sem=sem_core_s.at[i],
            recv_sem=sem_core_r.at[place],
            device_id=at(y, z, 1 - core),
            device_id_type=MESH,
        ).wait_recv()
        chip_sum[i] = (terms[core, place].astype(F32) + from_core[place].astype(F32)).astype(BF16)
        for k in range(1, ny):
            target = lax.rem(y + k, ny)
            copy = pltpu.make_async_remote_copy(
                src_ref=chip_sum.at[i, target],
                dst_ref=from_y.at[i, k - 1],
                send_sem=sem_y_s.at[i, k - 1],
                recv_sem=sem_y_r.at[i, k - 1],
                device_id=at(target, z, core),
                device_id_type=MESH,
            )
            copy.start()
            y_copies.append(copy)
    last = None
    for i, k in enumerate(order):
        for j in range(ny - 1):
            y_copies[i * (ny - 1) + j].wait_recv()
        total = chip_sum[i, y].astype(F32)
        for j in range(ny - 1):
            total = total + from_y[i, j].astype(F32)
        if k == 0:
            last = total
        else:
            y_sum[i] = total.astype(BF16)
            copy = pltpu.make_async_remote_copy(
                src_ref=y_sum.at[i],
                dst_ref=from_z.at[k - 1],
                send_sem=sem_z_s.at[k - 1],
                recv_sem=sem_z_r.at[k - 1],
                device_id=at(y, places[i], core),
                device_id_type=MESH,
            )
            copy.start()
            z_copies.append(copy)
    for copy in z_copies:
        copy.wait_recv()
    for k in range(nz - 1):
        last = last + from_z[k].astype(F32)
    w1e[...] = last[0:a1]
    w2e[...] = last[a1:ra]
    w1n[...] = last[ra:rb]
    w2n[...] = last[rb : rb + b2]
    tail = last[rb + b2 : rb + b2 + 8]
    width = tail.shape[1]
    per = ge.shape[1]
    shifted = pltpu.roll(tail, lax.rem(width - per * dom, width), 1)
    ge[...] = shifted[0:1, 0:per]
    gn[...] = shifted[1:2, 0:per]
    for i, place in enumerate(places):
        pltpu.make_async_remote_copy(
            src_ref=terms.at[1 - core, place],
            dst_ref=from_core.at[place],
            send_sem=sem_core_s.at[i],
            recv_sem=sem_core_r.at[place],
            device_id=at(y, z, 1 - core),
            device_id_type=MESH,
        ).wait_send()
    for copy in y_copies + z_copies:
        copy.wait_send()


def reduced_terms(edge_terms, node_terms, gains):
    count = lax.axis_size("dom")
    nz = min(DOM_Z, count // 4)
    ny = count // (2 * nz)
    x_e, pre_e, act_e, out_e = edge_terms
    x_n, pre_n, act_n, out_n = node_terms
    hid, width = pre_e.shape[1], out_e.shape[1]
    rows = (x_e.shape[1] + 2 * hid + x_n.shape[1]) // count + 8
    vmem = pl.BlockSpec(memory_space=pltpu.VMEM)
    dma = pltpu.SemaphoreType.DMA
    return pl.pallas_call(
        functools.partial(reduce_kernel, (ny, nz)),
        out_shape=(
            jax.ShapeDtypeStruct((x_e.shape[1] // count, hid), F32),
            jax.ShapeDtypeStruct((hid // count, width), F32),
            jax.ShapeDtypeStruct((1, width // count), F32),
            jax.ShapeDtypeStruct((x_n.shape[1] // count, hid), F32),
            jax.ShapeDtypeStruct((hid // count, width), F32),
            jax.ShapeDtypeStruct((1, width // count), F32),
        ),
        in_specs=[vmem] * 9,
        out_specs=[vmem] * 6,
        scratch_shapes=[
            pltpu.VMEM((2, nz, ny, rows, width), BF16),
            pltpu.VMEM((nz, ny, rows, width), BF16),
            pltpu.VMEM((nz, ny, rows, width), BF16),
            pltpu.VMEM((nz, ny - 1, rows, width), BF16),
            pltpu.VMEM((nz, rows, width), BF16),
            pltpu.VMEM((nz - 1, rows, width), BF16),
            dma((nz,)),
            dma((nz,)),
            dma((nz, ny - 1)),
            dma((nz, ny - 1)),
            dma((nz - 1,)),
            dma((nz - 1,)),
        ],
        compiler_params=pltpu.CompilerParams(
            collective_id=0, has_side_effects=True, vmem_limit_bytes=60 * 1024 * 1024
        ),
        name="weight_reduce",
    )(x_e, pre_e, act_e, out_e, x_n, pre_n, act_n, out_n, gains)


def on_device(
    node_states, edge_states, node_cot, edge_cot,
    edge_w1, edge_w2, edge_gain, node_w1, node_w2, node_gain,
    edge_src, edge_dst, edge_count, send_rows,
):
    phases = lax.axis_size("pipe")
    section = lax.axis_index("pipe")
    nodes, width = node_states.shape[2], node_states.shape[3]
    edges = edge_states.shape[2]
    ew1, ew2, nw1, nw2 = edge_w1[0], edge_w2[0], node_w1[0], node_w2[0]
    egain, ngain = edge_gain[0].astype(F32), node_gain[0].astype(F32)
    live = (jnp.arange(edges, dtype=jnp.int32) < edge_count[0]).astype(F32)[:, None]
    outgoing = send_rows[0].reshape(-1)
    ghosts_n = outgoing.shape[0]
    is_top = section == phases - 1
    h = node_states[0, 0]
    e = edge_states[0, 0]
    pick_send = (outgoing[:, None] == jnp.arange(nodes)[None, :]).astype(BF16)
    pick_src = (edge_src[:, None] == jnp.arange(nodes + ghosts_n)[None, :]).astype(BF16)
    pick_dst = (edge_dst[:, None] == jnp.arange(nodes)[None, :]).astype(BF16)
    sent = dot(pick_send, h).astype(BF16)
    ghosts = lax.all_to_all(sent, "dom", split_axis=0, concat_axis=0, tiled=True)
    table = jnp.concatenate([h, ghosts], axis=0)
    x_e = jnp.concatenate(
        [e, dot(pick_src, table).astype(BF16), dot(pick_dst, h).astype(BF16)], axis=1
    )
    act_e, slope_e, normed_e, rescale_e = mlp_forward(dot(x_e, ew1), ew2)
    new_edges = (e.astype(F32) + normed_e * egain) * live
    agg = contract(pick_dst, new_edges.astype(BF16)).astype(BF16)
    x_n = jnp.concatenate([h, agg], axis=1)
    act_n, slope_n, normed_n, rescale_n = mlp_forward(dot(x_n, nw1), nw2)

    carried = jnp.zeros((nodes + edges, width), BF16)
    kept = None
    for tick in range(phases):
        valid = tick == phases - 1 - section
        if tick > 0:
            carried = passed_along(carried, "pipe", -1)
        cn = jnp.where(is_top, node_cot[0], carried[:nodes]).astype(F32)
        ce = jnp.where(is_top, edge_cot[0], carried[nodes:]).astype(F32)
        out_n, pre_n, gain_n = mlp_backward(nw2, ngain, slope_n, normed_n, rescale_n, cn)
        back_n = dot_t(pre_n, nw1)
        g_edges = (ce + dot(pick_dst, back_n[:, width:].astype(BF16))) * live
        out_e, pre_e, gain_e = mlp_backward(ew2, egain, slope_e, normed_e, rescale_e, g_edges)
        by_src = dot_t(contract(pick_src, pre_e).astype(BF16), ew1[width : 2 * width])
        by_dst = dot_t(contract(pick_dst, pre_e).astype(BF16), ew1[2 * width :])
        edge_out = (g_edges + dot_t(pre_e, ew1[:width])).astype(BF16)
        back = lax.all_to_all(
            by_src[nodes:].astype(BF16), "dom", split_axis=0, concat_axis=0, tiled=True
        )
        node_out = (
            cn + back_n[:, :width] + by_dst + by_src[:nodes] + contract(pick_send, back)
        ).astype(BF16)
        carried = jnp.concatenate([node_out, edge_out], axis=0)
        gains = jnp.concatenate([gain_e, gain_n, jnp.zeros((6, width), F32)], axis=0)
        now = (node_out, edge_out, out_n, pre_n, out_e, pre_e, gains)
        if kept is None:
            kept = now
        else:
            kept = tuple(jnp.where(valid, a, b) for a, b in zip(now, kept))
    node_out, edge_out, out_n, pre_n, out_e, pre_e, gains = kept
    w1e, w2e, ge, w1n, w2n, gn = reduced_terms(
        (x_e, pre_e, act_e, out_e), (x_n, pre_n, act_n, out_n), gains
    )
    return (
        node_out[None, None], edge_out[None, None],
        w1e[None], w2e[None], ge, w1n[None], w2n[None], gn,
    )


def solution(mesh):
    placed = (
        P("pipe", None, "dom", None),
        P("pipe", None, "dom", None),
        P(None, "dom", None),
        P(None, "dom", None),
        P("pipe", None, None),
        P("pipe", None, None),
        P("pipe", None),
        P("pipe", None, None),
        P("pipe", None, None),
        P("pipe", None),
        P("dom"),
        P("dom"),
        P("dom"),
        P("dom", None, None),
    )
    return jax.shard_map(
        on_device,
        mesh=mesh,
        in_specs=placed,
        out_specs=(
            P("pipe", None, "dom", None),
            P("pipe", None, "dom", None),
            P("pipe", "dom", None),
            P("pipe", "dom", None),
            P("pipe", "dom"),
            P("pipe", "dom", None),
            P("pipe", "dom", None),
            P("pipe", "dom"),
        ),
        check_vma=False,
    )
```

```python
import functools

import jax
import jax.numpy as jnp
from jax import lax
from jax.experimental import pallas as pl
from jax.experimental.pallas import tpu as pltpu
from jax.sharding import PartitionSpec as P

EPS = 1e-05
MESH = pl.DeviceIdType.MESH
F32 = jnp.float32
BF16 = jnp.bfloat16
DOM_Z = 8
DOM_CORE = 2


def dot(a, b):
    return jnp.dot(a, b, preferred_element_type=F32)


def dot_t(a, b):
    return lax.dot_general(a, b, (((1,), (1,)), ((), ())), preferred_element_type=F32)


def contract(a, b):
    return lax.dot_general(a, b, (((0,), (0,)), ((), ())), preferred_element_type=F32)


def mean(x):
    return jnp.mean(x, axis=-1, keepdims=True)


def one_hot(rows, index):
    places = lax.broadcasted_iota(jnp.int32, (rows, index.shape[1]), 0)
    return jnp.where(places == index, 1.0, 0.0).astype(BF16)


def mlp_forward(pre, outer):
    sig = jax.nn.sigmoid(pre)
    act = (pre * sig).astype(BF16)
    out = dot(act, outer)
    centred = out - mean(out)
    rescale = lax.rsqrt(mean(centred * centred) + EPS)
    slope = sig * (1.0 + pre * (1.0 - sig))
    return act, slope, centred * rescale, rescale


def mlp_backward(outer, gain, slope, normed, rescale, cotangent):
    grad_norm = cotangent * gain
    grad_out = rescale * (grad_norm - mean(grad_norm) - normed * mean(grad_norm * normed))
    grad_out = grad_out.astype(BF16)
    grad_pre = (dot_t(grad_out, outer) * slope).astype(BF16)
    return grad_out, grad_pre


def layer_kernel(
    dims,
    h_ref, e_ref, ncot_ref, ecot_ref, ew1, ew2, egain, nw1, nw2, ngain, src_ref, dst_ref, count_ref, out_ref,
    node_out, edge_out, w1e, w2e, ge, w1n, w2n, gn,
    rows_f32, send_a, recv_a, send_b, recv_b, node_in, edge_in,
    terms, from_core, chip_sum, from_y, y_sum, from_z,
    sem_a, sem_b, sem_down, sem_up,
    sem_core_s, sem_core_r, sem_y_s, sem_y_r, sem_z_s, sem_z_r,
):
    phases, ny, nz = dims
    count = ny * nz * 2
    dom = lax.axis_index("dom")
    pipe = lax.axis_index("pipe")
    core = lax.rem(dom, 2)
    z = lax.rem(lax.div(dom, 2), nz)
    y = lax.div(dom, 2 * nz)
    nodes, width = h_ref.shape
    edges = e_ref.shape[0]

    def at(yy, zz, cc):
        return {"dom": (yy * nz + zz) * 2 + cc}

    barrier = pltpu.get_barrier_semaphore()

    def greet(k, carry):
        pl.semaphore_signal(
            barrier, inc=1, device_id={"dom": lax.rem(dom + k, count)}, device_id_type=MESH
        )
        return carry

    lax.fori_loop(1, count, greet, 0)
    pl.semaphore_signal(
        barrier, inc=1, device_id={"pipe": lax.rem(pipe + 1, phases)}, device_id_type=MESH
    )
    pl.semaphore_signal(
        barrier, inc=1, device_id={"pipe": lax.rem(pipe + phases - 1, phases)}, device_id_type=MESH
    )

    def spread(value, send):
        rows_f32[...] = value
        for q in range(count):
            send[q] = rows_f32[2 * q : 2 * q + 2].astype(BF16)

    def exchange(send, recv, sem):
        own = pltpu.make_async_copy(send.at[dom], recv.at[dom], sem.at[1])
        own.start()

        def go(k, carry):
            target = lax.rem(dom + k, count)
            pltpu.make_async_remote_copy(
                src_ref=send.at[target],
                dst_ref=recv.at[dom],
                send_sem=sem.at[0],
                recv_sem=sem.at[1],
                device_id={"dom": target},
                device_id_type=MESH,
            ).start()
            return carry

        lax.fori_loop(1, count, go, 0)

    def arrived(recv, sem):
        pltpu.make_async_copy(recv, recv, sem.at[1]).wait()
        for q in range(count):
            rows_f32[2 * q : 2 * q + 2] = recv[q].astype(F32)
        return rows_f32[...].astype(BF16)

    def departed(send, sem):
        part = send.at[pl.ds(0, count - 1)]
        pltpu.make_async_copy(part, part, sem.at[0]).wait()

    h = h_ref[...]
    e = e_ref[...]
    to_send = one_hot(nodes, out_ref[...])
    by_dst = one_hot(nodes, dst_ref[...])
    by_src = one_hot(nodes + 2 * count, src_ref[...])
    spread(contract(to_send, h), send_a)
    pl.semaphore_wait(barrier, count + 1)
    exchange(send_a, recv_a, sem_a)

    live = jnp.where(
        lax.broadcasted_iota(jnp.int32, (edges, width), 0) < count_ref[...], 1.0, 0.0
    )
    gain_e = egain[...].astype(F32)
    gain_n = ngain[...].astype(F32)
    x_dst = contract(by_dst, h).astype(BF16)
    pick_dst = jnp.transpose(by_dst.astype(F32)).astype(BF16)
    pre_e = dot(e, ew1[0:width]) + dot(x_dst, ew1[2 * width : 3 * width])
    ghosts = arrived(recv_a, sem_a)
    x_src = contract(by_src, jnp.concatenate([h, ghosts], axis=0)).astype(BF16)
    pre_e = pre_e + dot(x_src, ew1[width : 2 * width])
    act_e, slope_e, normed_e, rescale_e = mlp_forward(pre_e, ew2[...])
    new_edges = (e.astype(F32) + normed_e * gain_e) * live
    agg = dot(by_dst, new_edges.astype(BF16)).astype(BF16)
    pre_n = dot(h, nw1[0:width]) + dot(agg, nw1[width : 2 * width])
    act_n, slope_n, normed_n, rescale_n = mlp_forward(pre_n, nw2[...])

    below = {"pipe": lax.rem(pipe + phases - 1, phases)}
    node_down = pltpu.make_async_remote_copy(
        src_ref=node_out, dst_ref=node_in, send_sem=sem_down.at[0], recv_sem=sem_down.at[1],
        device_id=below, device_id_type=MESH,
    )
    edge_down = pltpu.make_async_remote_copy(
        src_ref=edge_out, dst_ref=edge_in, send_sem=sem_up.at[0], recv_sem=sem_up.at[1],
        device_id=below, device_id_type=MESH,
    )

    @pl.when(pipe == phases - 1)
    def _():
        node_in[...] = ncot_ref[...]
        edge_in[...] = ecot_ref[...]

    @pl.when(pipe < phases - 1)
    def _():
        node_down.wait_recv()

    cot_n = node_in[...].astype(F32)
    g_out_n, g_pre_n = mlp_backward(nw2[...], gain_n, slope_n, normed_n, rescale_n, cot_n)
    back_agg = dot_t(g_pre_n, nw1[width : 2 * width]).astype(BF16)
    picked = dot(pick_dst, back_agg)

    @pl.when(pipe < phases - 1)
    def _():
        edge_down.wait_recv()

    g_edges = (edge_in[...].astype(F32) + picked) * live
    g_out_e, g_pre_e = mlp_backward(ew2[...], gain_e, slope_e, normed_e, rescale_e, g_edges)
    pre_src = dot(by_src, g_pre_e).astype(BF16)
    spread(dot_t(pre_src[nodes:], ew1[width : 2 * width]), send_b)
    exchange(send_b, recv_b, sem_b)
    edge_out[...] = (g_edges + dot_t(g_pre_e, ew1[0:width])).astype(BF16)

    @pl.when(pipe > 0)
    def _():
        edge_down.start()

    pre_dst = dot(by_dst, g_pre_e).astype(BF16)
    node_part = (
        cot_n
        + dot_t(g_pre_n, nw1[0:width])
        + dot_t(pre_src[:nodes], ew1[width : 2 * width])
        + dot_t(pre_dst, ew1[2 * width : 3 * width])
    )

    a1, b1 = w1e.shape[0], w1n.shape[0]
    a2, b2 = w2e.shape[0], w2n.shape[0]
    gain_rows = jnp.concatenate(
        [
            jnp.sum(g_edges * normed_e, axis=0, keepdims=True),
            jnp.sum(cot_n * normed_n, axis=0, keepdims=True),
            jnp.zeros((6, width), F32),
        ],
        axis=0,
    )
    e1 = jnp.concatenate(
        [contract(e, g_pre_e), contract(x_src, g_pre_e), contract(x_dst, g_pre_e)], axis=0
    )
    e2 = contract(act_e, g_out_e)
    n1 = jnp.concatenate([contract(h, g_pre_n), contract(agg, g_pre_n)], axis=0)
    n2 = contract(act_n, g_out_n)
    ra = a1 + a2
    rb = ra + b1
    for d in range(count):
        c, yz = d % 2, d // 2
        yy, zz = yz // nz, yz % nz
        terms[c, zz, yy, 0:ra] = jnp.concatenate(
            [e1[a1 * d : a1 * d + a1], e2[a2 * d : a2 * d + a2]], axis=0
        ).astype(BF16)
        terms[c, zz, yy, ra:rb] = n1[b1 * d : b1 * d + b1].astype(BF16)
        terms[c, zz, yy, rb : rb + b2 + 8] = jnp.concatenate(
            [n2[b2 * d : b2 * d + b2], gain_rows], axis=0
        ).astype(BF16)

    order = sorted(range(nz), key=lambda k: -min(k, nz - k))
    places = [lax.rem(z + k, nz) for k in order]
    core_copies, y_copies, z_copies = [], [], []
    for i, place in enumerate(places):
        copy = pltpu.make_async_remote_copy(
            src_ref=terms.at[1 - core, place],
            dst_ref=from_core.at[i],
            send_sem=sem_core_s.at[i],
            recv_sem=sem_core_r.at[i],
            device_id=at(y, z, 1 - core),
            device_id_type=MESH,
        )
        copy.start()
        core_copies.append(copy)

    back = arrived(recv_b, sem_b)
    node_out[...] = (node_part + dot(to_send, back)).astype(BF16)

    @pl.when(pipe > 0)
    def _():
        node_down.start()

    for i, place in enumerate(places):
        core_copies[i].wait_recv()
        chip_sum[i] = (terms[core, place].astype(F32) + from_core[i].astype(F32)).astype(BF16)
        for k in range(1, ny):
            target = lax.rem(y + k, ny)
            copy = pltpu.make_async_remote_copy(
                src_ref=chip_sum.at[i, target],
                dst_ref=from_y.at[i, k - 1],
                send_sem=sem_y_s.at[i, k - 1],
                recv_sem=sem_y_r.at[i, k - 1],
                device_id=at(target, z, core),
                device_id_type=MESH,
            )
            copy.start()
            y_copies.append(copy)
    last = None
    for i, k in enumerate(order):
        for j in range(ny - 1):
            y_copies[i * (ny - 1) + j].wait_recv()
        total = chip_sum[i, y].astype(F32)
        for j in range(ny - 1):
            total = total + from_y[i, j].astype(F32)
        if k == 0:
            last = total
        else:
            y_sum[i] = total.astype(BF16)
            copy = pltpu.make_async_remote_copy(
                src_ref=y_sum.at[i],
                dst_ref=from_z.at[k - 1],
                send_sem=sem_z_s.at[k - 1],
                recv_sem=sem_z_r.at[k - 1],
                device_id=at(y, places[i], core),
                device_id_type=MESH,
            )
            copy.start()
            z_copies.append(copy)
    for copy in z_copies:
        copy.wait_recv()
    for k in range(nz - 1):
        last = last + from_z[k].astype(F32)
    w1e[...] = last[0:a1]
    w2e[...] = last[a1:ra]
    w1n[...] = last[ra:rb]
    w2n[...] = last[rb : rb + b2]
    tail = last[rb + b2 : rb + b2 + 8]
    per = ge.shape[1]
    shifted = pltpu.roll(tail, lax.rem(width - per * dom, width), 1)
    ge[...] = shifted[0:1, 0:per]
    gn[...] = shifted[1:2, 0:per]
    departed(send_a, sem_a)
    departed(send_b, sem_b)

    @pl.when(pipe > 0)
    def _():
        node_down.wait_send()
        edge_down.wait_send()

    for copy in core_copies + y_copies + z_copies:
        copy.wait_send()


def on_device(
    node_states, edge_states, node_cot, edge_cot,
    edge_w1, edge_w2, edge_gain, node_w1, node_w2, node_gain,
    edge_src, edge_dst, edge_count, send_rows,
):
    phases = lax.axis_size("pipe")
    count = lax.axis_size("dom")
    nz = min(DOM_Z, count // 4)
    ny = count // (2 * nz)
    nodes, width = node_states.shape[2:]
    edges = edge_states.shape[2]
    hid = edge_w2.shape[1]
    a1, a2, b1 = edge_w1.shape[1] // count, hid // count, node_w1.shape[1] // count
    rows = a1 + 2 * a2 + b1 + 8
    vmem = pl.BlockSpec(memory_space=pltpu.VMEM)
    dma = pltpu.SemaphoreType.DMA

    def shape(*sizes, kind=F32):
        return jax.ShapeDtypeStruct(sizes, kind)

    node_out, edge_out, w1e, w2e, ge, w1n, w2n, gn = pl.pallas_call(
        functools.partial(layer_kernel, (phases, ny, nz)),
        out_shape=(
            shape(nodes, width, kind=BF16),
            shape(edges, width, kind=BF16),
            shape(a1, hid),
            shape(a2, width),
            shape(1, width // count),
            shape(b1, hid),
            shape(a2, width),
            shape(1, width // count),
        ),
        in_specs=[vmem] * 14,
        out_specs=[vmem] * 8,
        scratch_shapes=[
            pltpu.VMEM((2 * count, width), F32),
            pltpu.VMEM((count, 2, width), BF16),
            pltpu.VMEM((count, 2, width), BF16),
            pltpu.VMEM((count, 2, width), BF16),
            pltpu.VMEM((count, 2, width), BF16),
            pltpu.VMEM((nodes, width), BF16),
            pltpu.VMEM((edges, width), BF16),
            pltpu.VMEM((2, nz, ny, rows, width), BF16),
            pltpu.VMEM((nz, ny, rows, width), BF16),
            pltpu.VMEM((nz, ny, rows, width), BF16),
            pltpu.VMEM((nz, ny - 1, rows, width), BF16),
            pltpu.VMEM((nz, rows, width), BF16),
            pltpu.VMEM((nz - 1, rows, width), BF16),
            dma((2,)),
            dma((2,)),
            dma((2,)),
            dma((2,)),
            dma((nz,)),
            dma((nz,)),
            dma((nz, ny - 1)),
            dma((nz, ny - 1)),
            dma((nz - 1,)),
            dma((nz - 1,)),
        ],
        compiler_params=pltpu.CompilerParams(
            collective_id=0, has_side_effects=True, vmem_limit_bytes=60 * 1024 * 1024
        ),
        name="relay_backward",
    )(
        node_states[0, 0], edge_states[0, 0], node_cot[0], edge_cot[0],
        edge_w1[0], edge_w2[0], edge_gain, node_w1[0], node_w2[0], node_gain,
        edge_src[None], edge_dst[None], edge_count[None], send_rows.reshape(1, 2 * count),
    )
    return (
        node_out[None, None], edge_out[None, None],
        w1e[None], w2e[None], ge, w1n[None], w2n[None], gn,
    )


def solution(mesh):
    placed = (
        P("pipe", None, "dom", None),
        P("pipe", None, "dom", None),
        P(None, "dom", None),
        P(None, "dom", None),
        P("pipe", None, None),
        P("pipe", None, None),
        P("pipe", None),
        P("pipe", None, None),
        P("pipe", None, None),
        P("pipe", None),
        P("dom"),
        P("dom"),
        P("dom"),
        P("dom", None, None),
    )
    return jax.shard_map(
        on_device,
        mesh=mesh,
        in_specs=placed,
        out_specs=(
            P("pipe", None, "dom", None),
            P("pipe", None, "dom", None),
            P("pipe", "dom", None),
            P("pipe", "dom", None),
            P("pipe", "dom"),
            P("pipe", "dom", None),
            P("pipe", "dom", None),
            P("pipe", "dom"),
        ),
        check_vma=False,
    )
```

```python
import functools

import jax
import jax.numpy as jnp
from jax import lax
from jax.experimental import pallas as pl
from jax.experimental.pallas import tpu as pltpu
from jax.sharding import PartitionSpec as P

EPS = 1e-05
MESH = pl.DeviceIdType.MESH
F32 = jnp.float32
BF16 = jnp.bfloat16
DOM_Z = 8
DOM_CORE = 2


def dot(a, b):
    return jnp.dot(a, b, preferred_element_type=F32)


def dot_t(a, b):
    return lax.dot_general(a, b, (((1,), (1,)), ((), ())), preferred_element_type=F32)


def contract(a, b):
    return lax.dot_general(a, b, (((0,), (0,)), ((), ())), preferred_element_type=F32)


def mean(x):
    return jnp.mean(x, axis=-1, keepdims=True)


def far_first(size):
    return sorted(range(size), key=lambda k: -min(k, size - k))


def one_hot(rows, index):
    places = lax.broadcasted_iota(jnp.int32, (rows, index.shape[1]), 0)
    return jnp.where(places == index, 1.0, 0.0).astype(BF16)


def interleaved(pair):
    half = pair.shape[1]
    spot = lax.broadcasted_iota(jnp.int32, (half, 2 * half), 1)
    row = 2 * lax.broadcasted_iota(jnp.int32, (half, 2 * half), 0)
    even = jnp.where(spot == row, 1.0, 0.0).astype(BF16)
    odd = jnp.where(spot == row + 1, 1.0, 0.0).astype(BF16)
    pair = pair.astype(BF16)
    both = dot(pair[0:1], even) + dot(pair[1:2], odd)
    return (both + 0.5).astype(jnp.int32)


def mlp_forward(pre, outer):
    sig = jax.nn.sigmoid(pre)
    act = (pre * sig).astype(BF16)
    out = dot(act, outer)
    centred = out - mean(out)
    rescale = lax.rsqrt(mean(centred * centred) + EPS)
    slope = sig * (1.0 + pre * (1.0 - sig))
    return act, slope, centred * rescale, rescale


def mlp_backward(outer, gain, slope, normed, rescale, cotangent):
    grad_norm = cotangent * gain
    grad_out = rescale * (grad_norm - mean(grad_norm) - normed * mean(grad_norm * normed))
    grad_out = grad_out.astype(BF16)
    grad_pre = (dot_t(grad_out, outer) * slope).astype(BF16)
    return grad_out, grad_pre


def layer_kernel(
    dims,
    h_ref, e_ref, ncot_hbm, ecot_hbm, ew1_hbm, ew2_hbm, egain, nw1_hbm, nw2_hbm, ngain,
    src_ref, dst_ref, count_ref, out_ref,
    node_out, edge_out, w1e, w2e, ge, w1n, w2n, gn,
    ew1, ew2, nw1, nw2, sem_in,
    rows_f32, send_a, recv_a, send_b, recv_b, node_in, edge_in,
    terms, from_core, chip_sum, from_y, y_sum, from_z,
    sem_a, sem_b, sem_down, sem_up,
    sem_core_s, sem_core_r, sem_y_s, sem_y_r, sem_z_s, sem_z_r,
):
    phases, ny, nz = dims
    count = ny * nz * 2
    dom = lax.axis_index("dom")
    pipe = lax.axis_index("pipe")
    core = lax.rem(dom, 2)
    z = lax.rem(lax.div(dom, 2), nz)
    y = lax.div(dom, 2 * nz)
    nodes, width = h_ref.shape
    edges = e_ref.shape[0]

    def at(yy, zz, cc):
        return {"dom": (yy * nz + zz) * 2 + cc}

    barrier = pltpu.get_barrier_semaphore()

    def greet(k, carry):
        pl.semaphore_signal(
            barrier, inc=1, device_id={"dom": lax.rem(dom + k, count)}, device_id_type=MESH
        )
        return carry

    lax.fori_loop(1, count, greet, 0)
    pl.semaphore_signal(
        barrier, inc=1, device_id={"pipe": lax.rem(pipe + 1, phases)}, device_id_type=MESH
    )
    pl.semaphore_signal(
        barrier, inc=1, device_id={"pipe": lax.rem(pipe + phases - 1, phases)}, device_id_type=MESH
    )

    def spread(value, send):
        rows_f32[...] = value
        for q in range(count):
            send[q] = rows_f32[2 * q : 2 * q + 2].astype(BF16)

    def exchange(send, recv, sem):
        own = pltpu.make_async_copy(send.at[dom], recv.at[dom], sem.at[1])
        own.start()

        for dz in far_first(nz):
            for dy in far_first(ny):
                for dc in (1, 0):
                    if dz + dy + dc > 0:
                        target = (
                            lax.rem(y + dy, ny) * nz + lax.rem(z + dz, nz)
                        ) * 2 + lax.rem(core + dc, 2)
                        pltpu.make_async_remote_copy(
                            src_ref=send.at[target],
                            dst_ref=recv.at[dom],
                            send_sem=sem.at[0],
                            recv_sem=sem.at[1],
                            device_id={"dom": target},
                            device_id_type=MESH,
                        ).start()

    def arrived(recv, sem):
        pltpu.make_async_copy(recv, recv, sem.at[1]).wait()
        for q in range(count):
            rows_f32[2 * q : 2 * q + 2] = recv[q].astype(F32)
        return rows_f32[...].astype(BF16)

    def departed(send, sem):
        part = send.at[pl.ds(0, count - 1)]
        pltpu.make_async_copy(part, part, sem.at[0]).wait()

    loads = [
        pltpu.make_async_copy(source, target, sem_in.at[i])
        for i, (source, target) in enumerate(
            [(ew1_hbm, ew1), (ew2_hbm, ew2), (nw1_hbm, nw1), (nw2_hbm, nw2)]
        )
    ]
    for load in loads:
        load.start()
    cot_loads = [
        pltpu.make_async_copy(ncot_hbm, node_in, sem_in.at[4]),
        pltpu.make_async_copy(ecot_hbm, edge_in, sem_in.at[5]),
    ]

    @pl.when(pipe == phases - 1)
    def _():
        for load in cot_loads:
            load.start()

    h = h_ref[...]
    e = e_ref[...]
    to_send = one_hot(nodes, interleaved(out_ref[...].astype(F32)))
    by_dst = one_hot(nodes, dst_ref[...])
    by_src = one_hot(nodes + 2 * count, src_ref[...])
    spread(contract(to_send, h), send_a)
    pl.semaphore_wait(barrier, count + 1)
    exchange(send_a, recv_a, sem_a)

    for load in loads:
        load.wait()
    live = jnp.where(
        lax.broadcasted_iota(jnp.int32, (edges, width), 0) < count_ref[...], 1.0, 0.0
    )
    gain_e = egain[...].astype(F32)
    gain_n = ngain[...].astype(F32)
    x_dst = contract(by_dst, h).astype(BF16)
    pick_dst = jnp.transpose(by_dst.astype(F32)).astype(BF16)
    pre_e = dot(e, ew1[0:width]) + dot(x_dst, ew1[2 * width : 3 * width])
    ghosts = arrived(recv_a, sem_a)
    x_src = contract(by_src, jnp.concatenate([h, ghosts], axis=0)).astype(BF16)
    pre_e = pre_e + dot(x_src, ew1[width : 2 * width])
    act_e, slope_e, normed_e, rescale_e = mlp_forward(pre_e, ew2[...])
    new_edges = (e.astype(F32) + normed_e * gain_e) * live
    agg = dot(by_dst, new_edges.astype(BF16)).astype(BF16)
    pre_n = dot(h, nw1[0:width]) + dot(agg, nw1[width : 2 * width])
    act_n, slope_n, normed_n, rescale_n = mlp_forward(pre_n, nw2[...])

    below = {"pipe": lax.rem(pipe + phases - 1, phases)}
    node_down = pltpu.make_async_remote_copy(
        src_ref=node_out, dst_ref=node_in, send_sem=sem_down.at[0], recv_sem=sem_down.at[1],
        device_id=below, device_id_type=MESH,
    )
    edge_down = pltpu.make_async_remote_copy(
        src_ref=edge_out, dst_ref=edge_in, send_sem=sem_up.at[0], recv_sem=sem_up.at[1],
        device_id=below, device_id_type=MESH,
    )

    @pl.when(pipe == phases - 1)
    def _():
        for load in cot_loads:
            load.wait()

    @pl.when(pipe < phases - 1)
    def _():
        node_down.wait_recv()

    cot_n = node_in[...].astype(F32)
    g_out_n, g_pre_n = mlp_backward(nw2[...], gain_n, slope_n, normed_n, rescale_n, cot_n)
    back_agg = dot_t(g_pre_n, nw1[width : 2 * width]).astype(BF16)
    picked = dot(pick_dst, back_agg)

    @pl.when(pipe < phases - 1)
    def _():
        edge_down.wait_recv()

    g_edges = (edge_in[...].astype(F32) + picked) * live
    g_out_e, g_pre_e = mlp_backward(ew2[...], gain_e, slope_e, normed_e, rescale_e, g_edges)
    pre_src = dot(by_src, g_pre_e).astype(BF16)
    spread(dot_t(pre_src[nodes:], ew1[width : 2 * width]), send_b)
    exchange(send_b, recv_b, sem_b)
    edge_out[...] = (g_edges + dot_t(g_pre_e, ew1[0:width])).astype(BF16)

    @pl.when(pipe > 0)
    def _():
        edge_down.start()

    pre_dst = dot(by_dst, g_pre_e).astype(BF16)
    node_part = (
        cot_n
        + dot_t(g_pre_n, nw1[0:width])
        + dot_t(pre_src[:nodes], ew1[width : 2 * width])
        + dot_t(pre_dst, ew1[2 * width : 3 * width])
    )

    a1, b1 = w1e.shape[0], w1n.shape[0]
    a2, b2 = w2e.shape[0], w2n.shape[0]
    gain_rows = jnp.concatenate(
        [
            jnp.sum(g_edges * normed_e, axis=0, keepdims=True),
            jnp.sum(cot_n * normed_n, axis=0, keepdims=True),
            jnp.zeros((6, width), F32),
        ],
        axis=0,
    )
    e1 = jnp.concatenate(
        [contract(e, g_pre_e), contract(x_src, g_pre_e), contract(x_dst, g_pre_e)], axis=0
    )
    e2 = contract(act_e, g_out_e)
    n1 = jnp.concatenate([contract(h, g_pre_n), contract(agg, g_pre_n)], axis=0)
    n2 = contract(act_n, g_out_n)
    ra = a1 + a2
    rb = ra + b1
    for d in range(count):
        c, yz = d % 2, d // 2
        yy, zz = yz // nz, yz % nz
        terms[c, zz, yy, 0:ra] = jnp.concatenate(
            [e1[a1 * d : a1 * d + a1], e2[a2 * d : a2 * d + a2]], axis=0
        ).astype(BF16)
        terms[c, zz, yy, ra:rb] = n1[b1 * d : b1 * d + b1].astype(BF16)
        terms[c, zz, yy, rb : rb + b2 + 8] = jnp.concatenate(
            [n2[b2 * d : b2 * d + b2], gain_rows], axis=0
        ).astype(BF16)

    order = far_first(nz)
    places = [lax.rem(z + k, nz) for k in order]
    core_copies, y_copies, z_copies = [], [], []
    for i, place in enumerate(places):
        copy = pltpu.make_async_remote_copy(
            src_ref=terms.at[1 - core, place],
            dst_ref=from_core.at[i],
            send_sem=sem_core_s.at[i],
            recv_sem=sem_core_r.at[i],
            device_id=at(y, z, 1 - core),
            device_id_type=MESH,
        )
        copy.start()
        core_copies.append(copy)

    back = arrived(recv_b, sem_b)
    node_out[...] = (node_part + dot(to_send, back)).astype(BF16)

    @pl.when(pipe > 0)
    def _():
        node_down.start()

    for i, place in enumerate(places):
        core_copies[i].wait_recv()
        chip_sum[i] = (terms[core, place].astype(F32) + from_core[i].astype(F32)).astype(BF16)
        for k in range(1, ny):
            target = lax.rem(y + k, ny)
            copy = pltpu.make_async_remote_copy(
                src_ref=chip_sum.at[i, target],
                dst_ref=from_y.at[i, k - 1],
                send_sem=sem_y_s.at[i, k - 1],
                recv_sem=sem_y_r.at[i, k - 1],
                device_id=at(target, z, core),
                device_id_type=MESH,
            )
            copy.start()
            y_copies.append(copy)
    last = None
    for i, k in enumerate(order):
        for j in range(ny - 1):
            y_copies[i * (ny - 1) + j].wait_recv()
        total = chip_sum[i, y].astype(F32)
        for j in range(ny - 1):
            total = total + from_y[i, j].astype(F32)
        if k == 0:
            last = total
        else:
            y_sum[i] = total.astype(BF16)
            copy = pltpu.make_async_remote_copy(
                src_ref=y_sum.at[i],
                dst_ref=from_z.at[k - 1],
                send_sem=sem_z_s.at[k - 1],
                recv_sem=sem_z_r.at[k - 1],
                device_id=at(y, places[i], core),
                device_id_type=MESH,
            )
            copy.start()
            z_copies.append(copy)
    for copy in z_copies:
        copy.wait_recv()
    for k in range(nz - 1):
        last = last + from_z[k].astype(F32)
    w1e[...] = last[0:a1]
    w2e[...] = last[a1:ra]
    w1n[...] = last[ra:rb]
    w2n[...] = last[rb : rb + b2]
    tail = last[rb + b2 : rb + b2 + 8]
    per = ge.shape[1]
    shifted = pltpu.roll(tail, lax.rem(width - per * dom, width), 1)
    ge[...] = shifted[0:1, 0:per]
    gn[...] = shifted[1:2, 0:per]
    departed(send_a, sem_a)
    departed(send_b, sem_b)

    @pl.when(pipe > 0)
    def _():
        node_down.wait_send()
        edge_down.wait_send()

    for copy in core_copies + y_copies + z_copies:
        copy.wait_send()


def handed_on(*refs):
    half = len(refs) // 2
    for source, target in zip(refs[:half], refs[half:]):
        target[...] = source[...]


def on_device(
    node_states, edge_states, node_cot, edge_cot,
    edge_w1, edge_w2, edge_gain, node_w1, node_w2, node_gain,
    edge_src, edge_dst, edge_count, send_rows,
):
    phases = lax.axis_size("pipe")
    count = lax.axis_size("dom")
    nz = min(DOM_Z, count // 4)
    ny = count // (2 * nz)
    nodes, width = node_states.shape[2:]
    edges = edge_states.shape[2]
    hid = edge_w2.shape[1]
    a1, a2, b1 = edge_w1.shape[1] // count, hid // count, node_w1.shape[1] // count
    rows = a1 + 2 * a2 + b1 + 8
    vmem = pl.BlockSpec(memory_space=pltpu.VMEM)
    hbm = pl.BlockSpec(memory_space=pl.ANY)
    dma = pltpu.SemaphoreType.DMA

    def shape(*sizes, kind=F32):
        return jax.ShapeDtypeStruct(sizes, kind)

    results = pl.pallas_call(
        functools.partial(layer_kernel, (phases, ny, nz)),
        out_shape=(
            shape(nodes, width, kind=BF16),
            shape(edges, width, kind=BF16),
            shape(a1, hid),
            shape(a2, width),
            shape(1, width // count),
            shape(b1, hid),
            shape(a2, width),
            shape(1, width // count),
        ),
        in_specs=[vmem] * 2 + [hbm] * 4 + [vmem] + [hbm] * 2 + [vmem] * 5,
        out_specs=[vmem] * 8,
        scratch_shapes=[
            pltpu.VMEM(edge_w1.shape[1:], BF16),
            pltpu.VMEM(edge_w2.shape[1:], BF16),
            pltpu.VMEM(node_w1.shape[1:], BF16),
            pltpu.VMEM(node_w2.shape[1:], BF16),
            dma((6,)),
            pltpu.VMEM((2 * count, width), F32),
            pltpu.VMEM((count, 2, width), BF16),
            pltpu.VMEM((count, 2, width), BF16),
            pltpu.VMEM((count, 2, width), BF16),
            pltpu.VMEM((count, 2, width), BF16),
            pltpu.VMEM((nodes, width), BF16),
            pltpu.VMEM((edges, width), BF16),
            pltpu.VMEM((2, nz, ny, rows, width), BF16),
            pltpu.VMEM((nz, ny, rows, width), BF16),
            pltpu.VMEM((nz, ny, rows, width), BF16),
            pltpu.VMEM((nz, ny - 1, rows, width), BF16),
            pltpu.VMEM((nz, rows, width), BF16),
            pltpu.VMEM((nz - 1, rows, width), BF16),
            dma((2,)),
            dma((2,)),
            dma((2,)),
            dma((2,)),
            dma((nz,)),
            dma((nz,)),
            dma((nz, ny - 1)),
            dma((nz, ny - 1)),
            dma((nz - 1,)),
            dma((nz - 1,)),
        ],
        compiler_params=pltpu.CompilerParams(
            collective_id=0, has_side_effects=True, vmem_limit_bytes=60 * 1024 * 1024
        ),
        name="relay_backward",
    )(
        node_states[0, 0], edge_states[0, 0], node_cot[0], edge_cot[0],
        edge_w1[0], edge_w2[0], edge_gain, node_w1[0], node_w2[0], node_gain,
        edge_src[None], edge_dst[None], edge_count[None], send_rows[0].T,
    )
    node_out, edge_out, w1e, w2e, ge, w1n, w2n, gn = pl.pallas_call(
        handed_on,
        out_shape=tuple(jax.ShapeDtypeStruct(r.shape, r.dtype) for r in results),
        in_specs=[vmem] * 8,
        out_specs=[vmem] * 8,
        name="results",
    )(*results)
    return (
        node_out[None, None], edge_out[None, None],
        w1e[None], w2e[None], ge, w1n[None], w2n[None], gn,
    )


def solution(mesh):
    placed = (
        P("pipe", None, "dom", None),
        P("pipe", None, "dom", None),
        P(None, "dom", None),
        P(None, "dom", None),
        P("pipe", None, None),
        P("pipe", None, None),
        P("pipe", None),
        P("pipe", None, None),
        P("pipe", None, None),
        P("pipe", None),
        P("dom"),
        P("dom"),
        P("dom"),
        P("dom", None, None),
    )
    return jax.shard_map(
        on_device,
        mesh=mesh,
        in_specs=placed,
        out_specs=(
            P("pipe", None, "dom", None),
            P("pipe", None, "dom", None),
            P("pipe", "dom", None),
            P("pipe", "dom", None),
            P("pipe", "dom"),
            P("pipe", "dom", None),
            P("pipe", "dom", None),
            P("pipe", "dom"),
        ),
        check_vma=False,
    )
```
